256 devices in a mesh: lat: 8 (over z_hi, core), lon: 32 (over y, z_lo, x).
Axes of the slice: x: 4, y: 4, z: 8 (z_hi: 4, z_lo: 2; z = z_hi * 2 + z_lo), core: 2. Of those that a mesh axis runs over, the one named last changes fastest.
Arguments:
- grid_field: bfloat16 [256, 512, 640], P('lat', 'lon'), may hold values from -6 to 6
- conv_weight: float32 [2, 640, 4], replicated, may hold values from -6 to 6
- norm_gain: float32 [2, 640], replicated, may hold values from 0.1 to 1.9
- proj_in: bfloat16 [2, 640, 1280], replicated, may hold values from -0.25 to 0.25
- bias_in: float32 [2, 1280], replicated, may hold values from -3 to 3
- proj_out: bfloat16 [2, 1280, 640], replicated, may hold values from -0.15625 to 0.15625
- bias_out: float32 [2, 640], replicated, may hold values from -3 to 3
Outputs:
- next_field: bfloat16 [256, 512, 640], P('lat', 'lon')
The draws below stay inside these ranges and needn't reach their ends.
All inputs are finite; a program needn't handle non-finite values.
Results may differ from the reference program's by a relative error of at most 0.012.
Values may be sent and summed in bfloat16 or wider, within the bound.
No kernel may reach another device: no remote copies, remote signals or barrier semaphores. Data moves between devices by JAX's collectives and lax.ppermute only.
A program may use at most 64 MiB of HBM per device.

```python
import math
import jax
import jax.numpy as jnp
from jax import lax

C = 640
H = 1280
K = 4
NB = 2
LAT_DEV = 32
NLAT = 256
NLON = 512
N_LAT = 8


def shard_levels(rng, dims, pieces, smallest, top_value):
    factor_of, own = 1.0, jax.random.fold_in(rng, 6)
    for dim, shards_of in pieces:
        draws = jnp.exp(jax.random.uniform(jax.random.fold_in(own, dim), (shards_of,), jnp.float32, smallest / len(pieces), top_value / len(pieces)))
        factor_of = factor_of * jnp.repeat(draws, dims[dim] // shards_of).reshape([-1 if axis == dim else 1 for axis in range(len(dims))])
    return factor_of


def gaussian(own_key, shape, deviation, reach, pieces=(), kind=jnp.bfloat16):
    drawn = jax.random.normal(own_key, shape, jnp.float32) * deviation
    if len(pieces) > 0:
        drawn = shard_levels(own_key, shape, pieces, -0.22, 0.18) * drawn
    return jnp.clip(drawn, min=-reach, max=reach).astype(kind)


def setup_inputs(seed: int = 0) -> dict:
    key_of = jax.random.split(jax.random.key(seed), 8)
    return {
        "grid_field": gaussian(key_of[0], (NLAT, NLON, C), 1.0, 6.0, ((0, 8), (1, 32))),
        "conv_weight": gaussian(key_of[1], (NB, C, K), 1.0, 6.0, (), jnp.float32),
        "norm_gain": jnp.clip(1.0 + 0.18 * jax.random.normal(key_of[2], (NB, C), jnp.float32), 0.1, 1.9),
        "proj_in": gaussian(key_of[3], (NB, C, H), C ** -0.5, 0.25),
        "bias_in": gaussian(key_of[4], (NB, H), 0.5, 3.0, (), jnp.float32),
        "proj_out": gaussian(key_of[5], (NB, H, C), H ** -0.5, 0.15625),
        "bias_out": gaussian(key_of[6], (NB, C), 0.5, 3.0, (), jnp.float32),
    }


lat_reach = 3
lon_reach = 7
norm_eps = 1e-05

def basis_table(row_index, lat_count, lon_count):
    lat_step = math.pi / lat_count
    reach_radius = (lat_reach + 0.5) * lat_step
    colatitude = (row_index + 0.5) * lat_step
    lat_offset = (jnp.arange(2 * lat_reach + 1) - lat_reach).astype(jnp.float32)
    lon_offset = (jnp.arange(2 * lon_reach + 1) - lon_reach).astype(jnp.float32)
    lat_part = (lat_offset * (lat_step / reach_radius))[None, :, None]
    lon_part = lon_offset[None, None, :] * jnp.sin(colatitude)[:, None, None] * (2.0 * math.pi / lon_count / reach_radius)
    radius = jnp.sqrt(lat_part * lat_part + lon_part * lon_part)
    area_weight = jnp.abs(jnp.sin(colatitude[:, None, None] + lat_offset[None, :, None] * lat_step))
    inner_hat = jnp.maximum(0.0, 1.0 - radius)
    cycle_hat = jnp.maximum(0.0, 1.0 - jnp.abs(2.0 * radius - 1.0))
    basis_values = jnp.stack([inner_hat, cycle_hat, 2.0 * lat_part * cycle_hat, 2.0 * lon_part * cycle_hat], axis=-1)
    basis_values = basis_values * area_weight[..., None]
    normalizer = lax.optimization_barrier(jnp.sum(inner_hat * area_weight, axis=(1, 2)))
    return basis_values / normalizer[:, None, None, None]

def mlp_branch(convolved, gain, proj_in, bias_in, proj_out, bias_out):
    flat_rows = convolved.reshape(-1, convolved.shape[-1]).astype(jnp.float32)
    channel_mean = lax.optimization_barrier(jnp.mean(flat_rows, axis=-1, keepdims=True))
    centered = flat_rows - channel_mean
    variance = lax.optimization_barrier(jnp.mean(centered * centered, axis=-1, keepdims=True))
    normed = (centered * lax.rsqrt(variance + norm_eps) * gain).astype(jnp.bfloat16)
    hidden = jax.nn.gelu(jnp.dot(normed, proj_in, preferred_element_type=jnp.float32) + bias_in, approximate=False).astype(jnp.bfloat16)
    output = jnp.dot(hidden, proj_out, preferred_element_type=jnp.float32) + bias_out
    return output.reshape(convolved.shape)

def reference(grid_field, conv_weight, norm_gain, proj_in, bias_in, proj_out, bias_out):
    current = grid_field
    for block_index in range(NB):
        padded = jnp.pad(current, ((lat_reach, lat_reach), (0, 0), (0, 0)))
        padded = jnp.concatenate([padded[:, NLON - lon_reach:], padded, padded[:, :lon_reach]], axis=1)

        def one_band(row_start):
            window = lax.dynamic_slice_in_dim(padded, row_start, LAT_DEV + 2 * lat_reach, 0)
            own_rows = lax.dynamic_slice_in_dim(current, row_start, LAT_DEV, 0)
            row_index = (row_start + jnp.arange(LAT_DEV).astype(jnp.int32)).astype(jnp.float32)
            filters = jnp.einsum('iabk,ck->abic', basis_table(row_index, NLAT, NLON), conv_weight[block_index], precision=lax.Precision.HIGHEST)
            summed = jnp.zeros((LAT_DEV, NLON, C), jnp.float32)
            for lat_tap in range(2 * lat_reach + 1):
                for lon_tap in range(2 * lon_reach + 1):
                    summed = summed + filters[lat_tap, lon_tap, :, None, :] * window[lat_tap:lat_tap + LAT_DEV, lon_tap:lon_tap + NLON, :]
            convolved = summed.astype(jnp.bfloat16)
            branch = mlp_branch(convolved, norm_gain[block_index], proj_in[block_index], bias_in[block_index], proj_out[block_index], bias_out[block_index])
            return (own_rows.astype(jnp.float32) + branch).astype(jnp.bfloat16)
        band_starts = (jnp.arange(N_LAT) * LAT_DEV).astype(jnp.int32)
        row_bands = lax.map(one_band, band_starts)
        current = row_bands.reshape(NLAT, NLON, C)
    return current
```

```python
import functools
import math

import jax
import jax.numpy as jnp
from jax import lax
from jax.experimental import pallas as pl
from jax.experimental.pallas import tpu as pltpu
from jax.sharding import PartitionSpec as P

LAT_REACH = 3
LON_REACH = 7
NORM_EPS = 1e-05
LAT_TAPS = 2 * LAT_REACH + 1
BASIS = 4
PAIR = 2
SPAN = PAIR + 2 * LAT_REACH
SIDE = 64


def row_tables(first_row, windows, side_start, lon_cells, lat_count, lon_count):
    lat_step = math.pi / lat_count
    reach_radius = (LAT_REACH + 0.5) * lat_step
    rows = first_row + jnp.arange(windows * PAIR).astype(jnp.float32)
    colatitude = (rows + 0.5) * lat_step
    lat_offset = (jnp.arange(LAT_TAPS) - LAT_REACH).astype(jnp.float32)
    lon_offset = (jnp.arange(2 * LON_REACH + 1) - LON_REACH).astype(jnp.float32)
    lon_scale = jnp.sin(colatitude) * (2.0 * math.pi / lon_count / reach_radius)
    lat_part = lat_offset * (lat_step / reach_radius)
    area = jnp.abs(jnp.sin(colatitude[:, None] + lat_offset[None, :] * lat_step))
    radius = jnp.sqrt(
        (lat_part * lat_part)[None, :, None] + (lon_offset[None, None, :] * lon_scale[:, None, None]) ** 2
    )
    normalizer = jnp.sum(jnp.maximum(0.0, 1.0 - radius) * area[:, :, None], axis=(1, 2))
    area = area / normalizer[:, None]

    own = jnp.arange(SPAN * lon_cells)
    own_row, own_lon = own // lon_cells, own % lon_cells
    starts = side_start + PAIR * LON_REACH * jnp.arange(windows)
    lead = starts % 8
    packed = jnp.arange(SIDE)[None, :] - lead[:, None]
    side_row = jnp.floor_divide(packed, LON_REACH)
    side_lon = packed - side_row * LON_REACH
    tile = lambda v: jnp.broadcast_to(v[None, :], (windows, v.shape[0]))
    span_row = jnp.concatenate([tile(own_row), side_row, side_row], axis=1)
    span_lon = jnp.concatenate(
        [tile(own_lon), side_lon - LON_REACH, side_lon + lon_cells], axis=1
    ).astype(jnp.float32)
    tap = span_row[:, None, :] - jnp.arange(PAIR)[None, :, None]
    inside = (tap >= 0) & (tap < LAT_TAPS) & (span_row >= 0)[:, None, :] & (span_row < SPAN)[:, None, :]
    area_of = jnp.zeros(tap.shape, jnp.float32)
    area = area.reshape(windows, PAIR, LAT_TAPS)
    for a in range(LAT_TAPS):
        area_of = jnp.where(inside & (tap == a), area[:, :, a : a + 1], area_of)
    lat_of = (tap.astype(jnp.float32) - LAT_REACH) * (lat_step / reach_radius)
    scale_of = jnp.broadcast_to(lon_scale.reshape(windows, PAIR, 1), tap.shape)
    lon_of = jnp.broadcast_to(span_lon[:, None, :], tap.shape)
    return jnp.stack([area_of, lat_of, scale_of, lon_of], axis=2).reshape(windows, PAIR * 4, tap.shape[-1])


def basis_kernel(lon_cells, table_ref, out_ref):
    def window(w, carry):
        for i in range(PAIR):
            area, lat_of, scale, lon = (table_ref[w, 4 * i + n : 4 * i + n + 1, :] for n in range(4))
            cell = lax.broadcasted_iota(jnp.int32, (lon_cells, table_ref.shape[2]), 0).astype(jnp.float32)
            offset = lon - cell
            lon_of = offset * scale
            area = jnp.where(jnp.abs(offset) < LON_REACH + 0.5, area, 0.0)
            radius = jnp.sqrt(lat_of * lat_of + lon_of * lon_of)
            inner = area * jnp.maximum(0.0, 1.0 - radius)
            cycle = area * jnp.maximum(0.0, 1.0 - jnp.abs(2.0 * radius - 1.0))
            parts = (inner, cycle, 2.0 * lat_of * cycle, 2.0 * lon_of * cycle)
            for k, part in enumerate(parts):
                row = (i * BASIS + k) * lon_cells
                out_ref[w, row : row + lon_cells, :] = part.astype(jnp.bfloat16)
        return carry

    lax.fori_loop(0, table_ref.shape[0], window, 0)


def basis_matrices(table, lon_cells):
    windows, _, columns = table.shape
    return pl.pallas_call(
        functools.partial(basis_kernel, lon_cells),
        out_shape=jax.ShapeDtypeStruct((windows, PAIR * BASIS * lon_cells, columns), jnp.bfloat16),
        name="basis",
    )(table)


def picker(rows, lead, lon_cells, lat_rows, left):
    shape = (rows, lat_rows * lon_cells)
    packed = lax.broadcasted_iota(jnp.int32, shape, 0) - lead
    cell = lax.broadcasted_iota(jnp.int32, shape, 1)
    row, lon = cell // lon_cells, cell % lon_cells
    lon = lon if left else lon - (lon_cells - LON_REACH)
    hit = (row * LON_REACH + lon == packed) & (lon >= 0) & (lon < LON_REACH)
    return jnp.where(hit, 1.0, 0.0).astype(jnp.bfloat16)


def pick(matrix, cells):
    return jnp.dot(matrix, cells, preferred_element_type=jnp.float32).astype(jnp.bfloat16)


def pack_kernel(lon_cells, above_ref, own_ref, below_ref, left_ref, right_ref):
    group = 8
    for left, ref in ((True, left_ref), (False, right_ref)):
        ext = above_ref.shape[0] // lon_cells
        edge = ext * LON_REACH
        room = -(-edge // 8) * 8
        ref[0:room, :] = pick(picker(room, room - edge, lon_cells, ext, left), above_ref[...])
        matrix = picker(group * LON_REACH, 0, lon_cells, group, left)
        count = own_ref.shape[0] // (group * lon_cells)
        for g in range(count):
            cells = own_ref[g * group * lon_cells : (g + 1) * group * lon_cells, :]
            at = room + g * group * LON_REACH
            ref[at : at + group * LON_REACH, :] = pick(matrix, cells)
        at = room + count * group * LON_REACH
        ref[at : at + room, :] = pick(picker(room, 0, lon_cells, ext, left), below_ref[...])


def pack_edges(above, own, below, lon_cells):
    room = -(-(above.shape[0] // lon_cells * LON_REACH) // 8) * 8
    rows = 2 * room + own.shape[0] // lon_cells * LON_REACH
    shape = jax.ShapeDtypeStruct((rows, own.shape[1]), own.dtype)
    return pl.pallas_call(
        functools.partial(pack_kernel, lon_cells), out_shape=(shape, shape), name="pack"
    )(above, own, below)


def gelu(z):
    return (0.5 * z) * (1.0 + lax.erf(z * math.sqrt(0.5)))


def block_kernel(
    block, lon_cells, side_start, mid, basis_ref, own_ref, left_ref, right_ref, mix_ref, gain_ref,
    bias_in_ref, bias_out_ref, proj_in_hbm, proj_out_hbm, *rest,
):
    if mid:
        out_ref, send_left_ref, send_right_ref, proj_in, proj_out, normed, hidden, sems = rest
    else:
        out_ref, proj_in, proj_out, normed, hidden, sems = rest
    load_in = pltpu.make_async_copy(proj_in_hbm.at[block], proj_in, sems.at[0])
    load_out = pltpu.make_async_copy(proj_out_hbm.at[block], proj_out, sems.at[1])
    load_in.start()
    load_out.start()
    windows = basis_ref.shape[0]
    cells = PAIR * lon_cells
    mix = [mix_ref[k : k + 1, :] for k in range(BASIS)]
    gain = gain_ref[...]

    def window(w, carry):
        own = own_ref[pl.ds(pl.multiple_of(w * cells, cells), SPAN * lon_cells), :]
        at = pl.multiple_of((side_start + w * PAIR * LON_REACH) // 8 * 8, 8)
        left = left_ref[pl.ds(at, SIDE), :]
        right = right_ref[pl.ds(at, SIDE), :]
        span = jnp.concatenate([own, left, right], axis=0)
        parts = jnp.dot(basis_ref[w], span, preferred_element_type=jnp.float32)
        for i in range(PAIR):
            conv = None
            for k in range(BASIS):
                row = (i * BASIS + k) * lon_cells
                term = parts[row : row + lon_cells, :] * mix[k]
                conv = term if conv is None else conv + term
            mean = jnp.mean(conv, axis=-1, keepdims=True)
            centered = conv - mean
            variance = jnp.mean(centered * centered, axis=-1, keepdims=True)
            value = centered * lax.rsqrt(variance + NORM_EPS) * gain
            to = pl.multiple_of(w * cells + i * lon_cells, lon_cells)
            normed[pl.ds(to, lon_cells), :] = value.astype(jnp.bfloat16)
        return carry

    lax.fori_loop(0, windows, window, 0)
    load_in.wait()
    load_out.wait()

    rows = windows * cells
    chunks = 2
    size = rows // chunks
    width = 256
    halo = LAT_REACH * lon_cells
    for m in range(chunks):
        lhs = normed[m * size : (m + 1) * size, :]
        for n in range(proj_in.shape[1] // width):
            at = slice(n * width, (n + 1) * width)
            z = jnp.dot(lhs, proj_in[:, at], preferred_element_type=jnp.float32) + bias_in_ref[:, at]
            hidden[m * size : (m + 1) * size, at] = gelu(z).astype(jnp.bfloat16)
        branch = jnp.dot(
            hidden[m * size : (m + 1) * size, :], proj_out[...], preferred_element_type=jnp.float32
        )
        own = own_ref[halo + m * size : halo + (m + 1) * size, :].astype(jnp.float32)
        out_ref[m * size : (m + 1) * size, :] = (own + (branch + bias_out_ref[...])).astype(jnp.bfloat16)

    if mid:
        lat = lax.axis_index("lat")
        for edge, at in ((0, 0), (lax.axis_size("lat") - 1, rows - halo)):
            @pl.when(lat == edge)
            def _():
                out_ref[at : at + halo, :] = jnp.zeros((halo, out_ref.shape[1]), jnp.bfloat16)
        group = 8
        for left, ref in ((True, send_left_ref), (False, send_right_ref)):
            for start in range(0, rows // lon_cells, group):
                size = min(group, rows // lon_cells - start)
                room = -(-size * LON_REACH // 8) * 8
                matrix = picker(room, 0, lon_cells, size, left)
                value = out_ref[start * lon_cells : (start + size) * lon_cells, :]
                ref[start * LON_REACH : start * LON_REACH + room, :] = pick(matrix, value)


def run_block(block, mid, basis, own, left, right, side_start, lon_cells, weights):
    mix, gain, bias_in, bias_out, proj_in, proj_out = weights
    windows = basis.shape[0]
    rows = windows * PAIR * lon_cells
    channels, hidden = proj_in.shape[1:]
    packed = -(-windows * PAIR * LON_REACH // 8) * 8
    out_shape = [jax.ShapeDtypeStruct((rows, channels), jnp.bfloat16)]
    if mid:
        out_shape += [jax.ShapeDtypeStruct((packed, channels), jnp.bfloat16)] * 2
    vmem = pl.BlockSpec(memory_space=pltpu.VMEM)
    return pl.pallas_call(
        functools.partial(block_kernel, block, lon_cells, side_start, mid),
        out_shape=out_shape,
        in_specs=[vmem] * 8 + [pl.BlockSpec(memory_space=pl.ANY)] * 2,
        out_specs=[vmem] * len(out_shape),
        scratch_shapes=[
            pltpu.VMEM((channels, hidden), jnp.bfloat16),
            pltpu.VMEM((hidden, channels), jnp.bfloat16),
            pltpu.VMEM((rows, channels), jnp.bfloat16),
            pltpu.VMEM((rows, hidden), jnp.bfloat16),
            pltpu.SemaphoreType.DMA((2,)),
        ],
        compiler_params=pltpu.CompilerParams(vmem_limit_bytes=48 << 20),
        name=f"block{block}",
    )(basis, own, left, right, mix[block], gain[block : block + 1], bias_in[block : block + 1],
      bias_out[block : block + 1], proj_in, proj_out)


def on_device(grid_field, conv_weight, norm_gain, proj_in, bias_in, proj_out, bias_out):
    lat_rows, lon_cells, channels = grid_field.shape
    lat_size, lon_size = lax.axis_size("lat"), lax.axis_size("lon")
    lat_count, lon_count = lat_rows * lat_size, lon_cells * lon_size
    row_start = (lax.axis_index("lat") * lat_rows).astype(jnp.float32)
    up = [(i, i + 1) for i in range(lat_size - 1)]
    down = [(j, i) for i, j in up]
    east = [(i, (i + 1) % lon_size) for i in range(lon_size)]
    west = [(j, i) for i, j in east]

    own = grid_field.reshape(lat_rows * lon_cells, channels)
    reach = 2 * LAT_REACH * lon_cells
    above = lax.ppermute(own[-reach:], "lat", up)
    below = lax.ppermute(own[:reach], "lat", down)
    edge = 2 * LAT_REACH * LON_REACH
    first_start = -edge % 8
    tables = [
        row_tables(row_start - LAT_REACH, lat_rows // PAIR + LAT_REACH, first_start, lon_cells, lat_count, lon_count),
        row_tables(row_start, lat_rows // PAIR, 0, lon_cells, lat_count, lon_count),
    ]
    to_west, to_east = pack_edges(above, own, below, lon_cells)
    left = lax.ppermute(to_east, "lon", east)
    right = lax.ppermute(to_west, "lon", west)
    basis = [basis_matrices(table, lon_cells) for table in tables]
    mix = jnp.swapaxes(conv_weight, 1, 2)
    weights = (mix, norm_gain, bias_in, bias_out, proj_in, proj_out)
    extended = jnp.concatenate([above, own, below], axis=0)
    current, to_west, to_east = run_block(
        0, True, basis[0], extended, left, right, first_start, lon_cells, weights
    )
    left = lax.ppermute(to_east, "lon", east)
    right = lax.ppermute(to_west, "lon", west)
    (result,) = run_block(1, False, basis[1], current, left, right, 0, lon_cells, weights)
    return result.reshape(grid_field.shape)


def solution(mesh):
    in_specs = (P("lat", "lon", None), P(), P(), P(), P(), P(), P())
    out_specs = P("lat", "lon", None)
    return jax.shard_map(
        on_device, mesh=mesh, in_specs=in_specs, out_specs=out_specs, check_vma=False
    )
```

```python
import functools
import math

import jax
import jax.numpy as jnp
from jax import lax
from jax.experimental import pallas as pl
from jax.experimental.pallas import tpu as pltpu
from jax.sharding import PartitionSpec as P

LAT_REACH = 3
LON_REACH = 7
NORM_EPS = 1e-05
LAT_TAPS = 2 * LAT_REACH + 1
BASIS = 4
PAIR = 2
SPAN = PAIR + 2 * LAT_REACH
SIDE = 64
SMALL = 6 << 20


def basis_kernel(lon_cells, first, side_start, lat_rows, after_ref, out_ref, sine_ref, scale_ref, area_ref):
    del after_ref
    windows, _, columns = out_ref.shape
    rows = scale_ref.shape[0]
    lat_step = math.pi / (lat_rows * lax.axis_size("lat"))
    lon_step = 2.0 * math.pi / (lon_cells * lax.axis_size("lon"))
    row_start = lax.axis_index("lat") * lat_rows + (first - LAT_REACH)
    row = (lax.broadcasted_iota(jnp.int32, sine_ref.shape, 0) + row_start).astype(jnp.float32)
    sine_ref[...] = jnp.sin((row + 0.5) * lat_step)
    scale = sine_ref[LAT_REACH : LAT_REACH + rows, :] * (lon_step / ((LAT_REACH + 0.5) * lat_step))
    scale_ref[...] = scale
    tap_lon = lax.broadcasted_iota(jnp.int32, scale.shape, 1)
    lon_of = (tap_lon - LON_REACH).astype(jnp.float32) * scale
    total = jnp.zeros(scale.shape, jnp.float32)
    for a in range(LAT_TAPS):
        lat_of = (a - LAT_REACH) / (LAT_REACH + 0.5)
        radius = jnp.sqrt(lat_of * lat_of + lon_of * lon_of)
        total = total + jnp.abs(sine_ref[a : a + rows, :]) * jnp.maximum(0.0, 1.0 - radius)
    total = jnp.where(tap_lon < 2 * LON_REACH + 1, total, 0.0)
    inverse = 1.0 / jnp.sum(total, axis=1, keepdims=True)
    for a in range(LAT_TAPS):
        area_ref[a] = jnp.abs(sine_ref[a : a + rows, :]) * inverse

    own = SPAN * lon_cells
    even = lax.axis_index("lon") % 2 == 0
    lon_of_near = jnp.where(even, lon_cells, -LON_REACH)
    lon_of_far = jnp.where(even, -LON_REACH, lon_cells)
    column = lax.broadcasted_iota(jnp.int32, (lon_cells, columns), 1)
    cell = lax.broadcasted_iota(jnp.int32, (lon_cells, columns), 0)
    is_own = column < own
    is_near = column < own + SIDE
    packed = jnp.where(is_near, column - own, column - (own + SIDE))
    side_base = jnp.where(is_near, lon_of_near, lon_of_far)
    own_row = column // lon_cells
    own_lon = column - own_row * lon_cells

    def window(w, carry):
        lead = (side_start + w * (PAIR * LON_REACH)) % 8
        place = packed - lead + LON_REACH
        side_row = place // LON_REACH - 1
        side_lon = place - (side_row + 1) * LON_REACH + side_base
        row = jnp.where(is_own, own_row, side_row)
        offset = (jnp.where(is_own, own_lon, side_lon) - cell).astype(jnp.float32)
        near = jnp.abs(offset) < LON_REACH + 0.5
        for i in range(PAIR):
            tap = row - i
            at = pl.ds(w * PAIR + i, 1)
            area = jnp.zeros(tap.shape, jnp.float32)
            for a in range(LAT_TAPS):
                area = jnp.where(tap == a, area_ref[a, at, :], area)
            area = jnp.where(near, area, 0.0)
            lat_of = (tap.astype(jnp.float32) - LAT_REACH) * (1.0 / (LAT_REACH + 0.5))
            lon_of = offset * scale_ref[at, :]
            radius = jnp.sqrt(lat_of * lat_of + lon_of * lon_of)
            inner = area * jnp.maximum(0.0, 1.0 - radius)
            cycle = area * jnp.maximum(0.0, 1.0 - jnp.abs(2.0 * radius - 1.0))
            parts = (inner, cycle, 2.0 * lat_of * cycle, 2.0 * lon_of * cycle)
            for k, part in enumerate(parts):
                to = (i * BASIS + k) * lon_cells
                out_ref[w, to : to + lon_cells, :] = part.astype(jnp.bfloat16)
        return carry

    lax.fori_loop(0, windows, window, 0)


def basis_matrices(after, first, windows, side_start, lat_rows, lon_cells):
    columns = SPAN * lon_cells + 2 * SIDE
    rows = -(-windows * PAIR // 8) * 8
    return pl.pallas_call(
        functools.partial(basis_kernel, lon_cells, first, side_start, lat_rows),
        out_shape=jax.ShapeDtypeStruct((windows, PAIR * BASIS * lon_cells, columns), jnp.bfloat16),
        in_specs=[pl.BlockSpec(memory_space=pl.ANY)],
        scratch_shapes=[
            pltpu.VMEM((rows + 8, columns), jnp.float32),
            pltpu.VMEM((rows, columns), jnp.float32),
            pltpu.VMEM((LAT_TAPS, rows, columns), jnp.float32),
        ],
        compiler_params=pltpu.CompilerParams(vmem_limit_bytes=SMALL),
        name="basis",
    )(after)


def lat_send_kernel(own_hbm, near_ref, far_ref, sems):
    size = near_ref.shape[0]
    last = own_hbm.shape[0] - size
    even = lax.axis_index("lat") % 2 == 0
    near_at = pl.multiple_of(jnp.where(even, last, 0), 8)
    far_at = pl.multiple_of(jnp.where(even, 0, last), 8)
    far = pltpu.make_async_copy(own_hbm.at[pl.ds(far_at, size)], far_ref, sems.at[0])
    near = pltpu.make_async_copy(own_hbm.at[pl.ds(near_at, size)], near_ref, sems.at[1])
    far.start()
    near.start()
    far.wait()
    near.wait()


def lat_send(own, size):
    shape = jax.ShapeDtypeStruct((size, own.shape[1]), own.dtype)
    return pl.pallas_call(
        lat_send_kernel, out_shape=(shape, shape), in_specs=[pl.BlockSpec(memory_space=pltpu.HBM)],
        scratch_shapes=[pltpu.SemaphoreType.DMA((2,))],
        compiler_params=pltpu.CompilerParams(vmem_limit_bytes=SMALL), name="lat_send",
    )(own)


def picker(rows, lead, lon_cells, lat_rows, east):
    shape = (rows, lat_rows * lon_cells)
    packed = lax.broadcasted_iota(jnp.int32, shape, 0) - lead
    cell = lax.broadcasted_iota(jnp.int32, shape, 1)
    row = cell // lon_cells
    lon = cell - row * lon_cells - jnp.where(east, lon_cells - LON_REACH, 0)
    hit = (row * LON_REACH + lon == packed) & (lon >= 0) & (lon < LON_REACH)
    return jnp.where(hit, 1.0, 0.0).astype(jnp.bfloat16)


def pick(matrix, cells):
    return jnp.dot(matrix, cells, preferred_element_type=jnp.float32).astype(jnp.bfloat16)


def pack_own_kernel(lon_cells, lead, own_ref, extended_ref, near_ref, far_ref):
    even = lax.axis_index("lon") % 2 == 0
    group = 16
    cells, packed = group * lon_cells, group * LON_REACH
    start = (extended_ref.shape[0] - own_ref.shape[0]) // 2
    extended_ref[start : start + own_ref.shape[0], :] = own_ref[...]
    for east, ref in ((even, near_ref), (jnp.logical_not(even), far_ref)):
        matrix = picker(packed, 0, lon_cells, group, east)
        for g in range(own_ref.shape[0] // cells):
            to = lead + g * packed
            ref[to : to + packed, :] = pick(matrix, own_ref[g * cells : (g + 1) * cells, :])


def pack_ends_kernel(
    lon_cells, far_lat_ref, near_lat_ref, extended_in, near_in, far_in, extended_ref, near_ref, far_ref
):
    del extended_in, near_in, far_in
    lat_even = lax.axis_index("lat") % 2 == 0
    even = lax.axis_index("lon") % 2 == 0
    size = near_lat_ref.shape[0]
    ext = size // lon_cells
    edge = ext * LON_REACH
    room = -(-edge // 8) * 8
    above = jnp.where(lat_even, far_lat_ref[...], near_lat_ref[...])
    below = jnp.where(lat_even, near_lat_ref[...], far_lat_ref[...])
    extended_ref[0:size, :] = above
    extended_ref[extended_ref.shape[0] - size :, :] = below
    for east, ref in ((even, near_ref), (jnp.logical_not(even), far_ref)):
        ref[0:room, :] = pick(picker(room, room - edge, lon_cells, ext, east), above)
        ref[ref.shape[0] - room :, :] = pick(picker(room, 0, lon_cells, ext, east), below)


def pack_own(own, ext_rows, lon_cells):
    room = -(-(ext_rows * LON_REACH) // 8) * 8
    rows = 2 * room + own.shape[0] // lon_cells * LON_REACH
    shape = jax.ShapeDtypeStruct((rows, own.shape[1]), own.dtype)
    extended = jax.ShapeDtypeStruct((own.shape[0] + 2 * ext_rows * lon_cells, own.shape[1]), own.dtype)
    return pl.pallas_call(
        functools.partial(pack_own_kernel, lon_cells, room), out_shape=(extended, shape, shape),
        compiler_params=pltpu.CompilerParams(vmem_limit_bytes=SMALL), name="pack_own",
    )(own)


def pack_ends(far_lat, near_lat, packed, lon_cells):
    return pl.pallas_call(
        functools.partial(pack_ends_kernel, lon_cells),
        out_shape=tuple(jax.ShapeDtypeStruct(v.shape, v.dtype) for v in packed),
        input_output_aliases={2: 0, 3: 1, 4: 2},
        compiler_params=pltpu.CompilerParams(vmem_limit_bytes=SMALL), name="pack_ends",
    )(far_lat, near_lat, *packed)


def gelu(z):
    return (0.5 * z) * (1.0 + lax.erf(z * math.sqrt(0.5)))


def block_kernel(
    block, lon_cells, side_start, mid, basis_ref, own_ref, side_far_ref, side_near_ref, mix_ref, gain_ref,
    bias_in_ref, bias_out_ref, proj_in_hbm, proj_out_hbm, *rest,
):
    if mid:
        out_ref, near_ref, far_ref, proj_in, proj_out, normed, hidden, sems = rest
    else:
        out_ref, proj_in, proj_out, normed, hidden, sems = rest
    load_in = pltpu.make_async_copy(proj_in_hbm.at[block], proj_in, sems.at[0])
    load_out = pltpu.make_async_copy(proj_out_hbm.at[block], proj_out, sems.at[1])
    load_in.start()
    load_out.start()
    windows = basis_ref.shape[0]
    cells = PAIR * lon_cells
    mix = [mix_ref[block, k : k + 1, :] for k in range(BASIS)]
    gain = gain_ref[block : block + 1, :]

    def window(w, carry):
        own = own_ref[pl.ds(pl.multiple_of(w * cells, cells), SPAN * lon_cells), :]
        at = pl.multiple_of((side_start + w * PAIR * LON_REACH) // 8 * 8, 8)
        near_side = side_near_ref[pl.ds(at, SIDE), :]
        far_side = side_far_ref[pl.ds(at, SIDE), :]
        span = jnp.concatenate([own, near_side, far_side], axis=0)
        parts = jnp.dot(basis_ref[w], span, preferred_element_type=jnp.float32)
        for i in range(PAIR):
            conv = None
            for k in range(BASIS):
                row = (i * BASIS + k) * lon_cells
                term = parts[row : row + lon_cells, :] * mix[k]
                conv = term if conv is None else conv + term
            mean = jnp.mean(conv, axis=-1, keepdims=True)
            centered = conv - mean
            variance = jnp.mean(centered * centered, axis=-1, keepdims=True)
            value = centered * lax.rsqrt(variance + NORM_EPS) * gain
            to = pl.multiple_of(w * cells + i * lon_cells, lon_cells)
            normed[pl.ds(to, lon_cells), :] = value.astype(jnp.bfloat16)
        return carry

    lax.fori_loop(0, windows, window, 0, unroll=windows)
    load_in.wait()
    load_out.wait()

    rows = windows * cells
    chunks = 2
    size = rows // chunks
    width = 256
    halo = LAT_REACH * lon_cells
    for m in range(chunks):
        lhs = normed[m * size : (m + 1) * size, :]
        for n in range(proj_in.shape[1] // width):
            at = slice(n * width, (n + 1) * width)
            z = jnp.dot(lhs, proj_in[:, at], preferred_element_type=jnp.float32) + bias_in_ref[block : block + 1, at]
            hidden[m * size : (m + 1) * size, at] = gelu(z).astype(jnp.bfloat16)
        branch = jnp.dot(
            hidden[m * size : (m + 1) * size, :], proj_out[...], preferred_element_type=jnp.float32
        )
        own = own_ref[halo + m * size : halo + (m + 1) * size, :].astype(jnp.float32)
        out_ref[m * size : (m + 1) * size, :] = (own + (branch + bias_out_ref[block : block + 1, :])).astype(jnp.bfloat16)

    if mid:
        lat = lax.axis_index("lat")
        for edge, at in ((0, 0), (lax.axis_size("lat") - 1, rows - halo)):
            @pl.when(lat == edge)
            def _():
                out_ref[at : at + halo, :] = jnp.zeros((halo, out_ref.shape[1]), jnp.bfloat16)
        even = lax.axis_index("lon") % 2 == 0
        for east, ref in ((even, near_ref), (jnp.logical_not(even), far_ref)):
            for start in range(0, rows // lon_cells, 16):
                size = min(16, rows // lon_cells - start)
                room = -(-size * LON_REACH // 8) * 8
                matrix = picker(room, 0, lon_cells, size, east)
                value = out_ref[start * lon_cells : (start + size) * lon_cells, :]
                ref[start * LON_REACH : start * LON_REACH + room, :] = pick(matrix, value)


def run_block(block, mid, basis, own, far, near, side_start, lon_cells, weights):
    mix, gain, bias_in, bias_out, proj_in, proj_out = weights
    windows = basis.shape[0]
    rows = windows * PAIR * lon_cells
    channels, hidden = proj_in.shape[1:]
    packed = -(-windows * PAIR * LON_REACH // 8) * 8
    out_shape = [jax.ShapeDtypeStruct((rows, channels), jnp.bfloat16)]
    if mid:
        out_shape += [jax.ShapeDtypeStruct((packed, channels), jnp.bfloat16)] * 2
    vmem = pl.BlockSpec(memory_space=pltpu.VMEM)
    return pl.pallas_call(
        functools.partial(block_kernel, block, lon_cells, side_start, mid),
        out_shape=out_shape,
        in_specs=[vmem] * 8 + [pl.BlockSpec(memory_space=pltpu.HBM)] * 2,
        out_specs=[vmem] * len(out_shape),
        scratch_shapes=[
            pltpu.VMEM((channels, hidden), jnp.bfloat16),
            pltpu.VMEM((hidden, channels), jnp.bfloat16),
            pltpu.VMEM((rows, channels), jnp.bfloat16),
            pltpu.VMEM((rows, hidden), jnp.bfloat16),
            pltpu.SemaphoreType.DMA((2,)),
        ],
        compiler_params=pltpu.CompilerParams(vmem_limit_bytes=16 << 20),
        name=f"block{block}",
    )(basis, own, far, near, mix, gain, bias_in, bias_out, proj_in, proj_out)


def on_device(grid_field, conv_weight, norm_gain, proj_in, bias_in, proj_out, bias_out):
    lat_rows, lon_cells, channels = grid_field.shape
    lat_size, lon_size = lax.axis_size("lat"), lax.axis_size("lon")
    swap = lambda pairs: [(i, j) for a, b in pairs for i, j in ((a, b), (b, a))]
    lat_near = swap([(i, i + 1) for i in range(0, lat_size, 2)])
    lat_far = swap([(i, i + 1) for i in range(1, lat_size - 1, 2)])
    lon_near = swap([(i, i + 1) for i in range(0, lon_size, 2)])
    lon_far = swap([(i, (i + 1) % lon_size) for i in range(1, lon_size, 2)])

    own = grid_field.reshape(lat_rows * lon_cells, channels)
    ext_rows = 2 * LAT_REACH
    reach = ext_rows * lon_cells
    in_hbm = lambda value: pltpu.with_memory_space_constraint(value, pltpu.HBM)
    near_lat, far_lat = lat_send(in_hbm(own), reach)
    far_lat = lax.ppermute(far_lat, "lat", lat_far)
    near_lat = lax.ppermute(near_lat, "lat", lat_near)
    packed = pack_own(own, ext_rows, lon_cells)
    extended, near_sent, far_sent = pack_ends(far_lat, near_lat, packed, lon_cells)
    far = lax.ppermute(far_sent, "lon", lon_far)
    near = lax.ppermute(near_sent, "lon", lon_near)
    first_start = -(ext_rows * LON_REACH) % 8
    first_windows, windows = lat_rows // PAIR + LAT_REACH, lat_rows // PAIR
    first_basis = basis_matrices(far_sent, -LAT_REACH, first_windows, first_start, lat_rows, lon_cells)
    basis = basis_matrices(far_sent, 0, windows, 0, lat_rows, lon_cells)
    mix = jnp.swapaxes(conv_weight, 1, 2)
    weights = (mix, norm_gain, bias_in, bias_out, in_hbm(proj_in), in_hbm(proj_out))
    current, near, far = run_block(0, True, first_basis, extended, far, near, first_start, lon_cells, weights)
    far = lax.ppermute(far, "lon", lon_far)
    near = lax.ppermute(near, "lon", lon_near)
    (result,) = run_block(1, False, basis, current, far, near, 0, lon_cells, weights)
    return result.reshape(grid_field.shape)


def solution(mesh):
    in_specs = (P("lat", "lon", None), P(), P(), P(), P(), P(), P())
    out_specs = P("lat", "lon", None)
    return jax.shard_map(
        on_device, mesh=mesh, in_specs=in_specs, out_specs=out_specs, check_vma=False
    )
```

```python
import functools
import math

import jax
import jax.numpy as jnp
from jax import lax
from jax.experimental import pallas as pl
from jax.experimental.pallas import tpu as pltpu
from jax.sharding import PartitionSpec as P

LAT_REACH = 3
LON_REACH = 7
NORM_EPS = 1e-05
LAT_TAPS = 2 * LAT_REACH + 1
BASIS = 4
HALF = 8
GROUP = 4
SPAN = GROUP + 2 * LAT_REACH
DEPTH = 256
SMALL = 8 << 20


def is_even(axis):
    return lax.axis_index(axis) % 2 == 0


def in_hbm(value):
    return pltpu.with_memory_space_constraint(value, pltpu.HBM)


def half_start(east):
    return jnp.where(east, HALF, 0)


def write_basis(first, lat_rows, near_ref, far_ref, sine_ref, scale_ref, area_ref):
    windows, _, columns = near_ref.shape
    rows = scale_ref.shape[0]
    lat_step = math.pi / (lat_rows * lax.axis_size("lat"))
    lon_step = 2.0 * math.pi / (2 * HALF * lax.axis_size("lon"))
    row_start = lax.axis_index("lat") * lat_rows + (first - LAT_REACH)
    row = (lax.broadcasted_iota(jnp.int32, sine_ref.shape, 0) + row_start).astype(jnp.float32)
    sine_ref[...] = jnp.sin((row + 0.5) * lat_step)
    scale = sine_ref[LAT_REACH : LAT_REACH + rows, :] * (lon_step / ((LAT_REACH + 0.5) * lat_step))
    scale_ref[...] = scale
    tap_lon = lax.broadcasted_iota(jnp.int32, scale.shape, 1)
    lon_of = (tap_lon - LON_REACH).astype(jnp.float32) * scale
    total = jnp.zeros(scale.shape, jnp.float32)
    for a in range(LAT_TAPS):
        lat_of = (a - LAT_REACH) / (LAT_REACH + 0.5)
        radius = jnp.sqrt(lat_of * lat_of + lon_of * lon_of)
        total = total + jnp.abs(sine_ref[a : a + rows, :]) * jnp.maximum(0.0, 1.0 - radius)
    total = jnp.where(tap_lon < 2 * LON_REACH + 1, total, 0.0)
    inverse = 1.0 / jnp.sum(total, axis=1, keepdims=True)
    for a in range(LAT_TAPS):
        area_ref[a] = jnp.abs(sine_ref[a : a + rows, :]) * inverse

    even = is_even("lon")
    odd = jnp.logical_not(even)
    column = lax.broadcasted_iota(jnp.int32, (HALF, columns), 1)
    cell = lax.broadcasted_iota(jnp.int32, (HALF, columns), 0)
    part = SPAN * HALF
    in_near, in_far = column < part, column < 2 * part
    local = jnp.where(in_near, column, jnp.where(in_far, column - part, column - 2 * part))
    span_row = local // HALF
    span_lon = local - span_row * HALF
    for ref, east in ((near_ref, even), (far_ref, odd)):
        beside = jnp.where(east, 2 * HALF, -HALF)
        base = jnp.where(in_near, half_start(even), jnp.where(in_far, half_start(odd), beside))
        offset = (span_lon + base - cell - half_start(east)).astype(jnp.float32)
        reach = jnp.abs(offset) < LON_REACH + 0.5

        def window(w, carry):
            for i in range(GROUP):
                tap = span_row - i
                at = pl.ds(w * GROUP + i, 1)
                area = jnp.zeros(tap.shape, jnp.float32)
                for a in range(LAT_TAPS):
                    area = jnp.where(tap == a, area_ref[a, at, :], area)
                area = jnp.where(reach, area, 0.0)
                lat_of = (tap.astype(jnp.float32) - LAT_REACH) * (1.0 / (LAT_REACH + 0.5))
                lon_of = offset * scale_ref[at, :]
                radius = jnp.sqrt(lat_of * lat_of + lon_of * lon_of)
                inner = area * jnp.maximum(0.0, 1.0 - radius)
                cycle = area * jnp.maximum(0.0, 1.0 - jnp.abs(2.0 * radius - 1.0))
                parts = (inner, cycle, 2.0 * lat_of * cycle, 2.0 * lon_of * cycle)
                for k, value in enumerate(parts):
                    to = (k * GROUP + i) * HALF
                    ref[w, to : to + HALF, :] = value.astype(jnp.bfloat16)
            return carry

        lax.fori_loop(0, windows, window, 0)


def prepare_kernel(
    first, lat_rows, after_ref, proj_in_hbm, proj_out_hbm, near_ref, far_ref, *rest,
):
    del after_ref
    *weights, sine_ref, scale_ref, area_ref, sems = rest
    copies = []
    for n, ref in enumerate(weights):
        hbm = (proj_in_hbm, proj_out_hbm)[n % 2]
        copies.append(pltpu.make_async_copy(hbm.at[n // 2], ref, sems.at[n]))
    for copy in copies:
        copy.start()
    write_basis(first, lat_rows, near_ref, far_ref, sine_ref, scale_ref, area_ref)
    for copy in copies:
        copy.wait()


def prepare(first, windows, lat_rows, after, proj_in, proj_out):
    rows = windows * GROUP
    matrix = jax.ShapeDtypeStruct((windows, BASIS * GROUP * HALF, DEPTH), jnp.bfloat16)
    blocks = proj_in.shape[0]
    weights = [jax.ShapeDtypeStruct(v.shape[1:], v.dtype) for _ in range(blocks) for v in (proj_in, proj_out)]
    return pl.pallas_call(
        functools.partial(prepare_kernel, first, lat_rows),
        out_shape=(matrix, matrix, *weights),
        in_specs=[pl.BlockSpec(memory_space=pl.ANY)] * 3,
        scratch_shapes=[
            pltpu.VMEM((rows + 8, DEPTH), jnp.float32),
            pltpu.VMEM((rows, DEPTH), jnp.float32),
            pltpu.VMEM((LAT_TAPS, rows, DEPTH), jnp.float32),
            pltpu.SemaphoreType.DMA((len(weights),)),
        ],
        compiler_params=pltpu.CompilerParams(vmem_limit_bytes=20 << 20),
        cost_estimate=pl.CostEstimate(flops=1 << 22, bytes_accessed=8 << 20, transcendentals=1 << 19),
        name="prepare",
    )(after, in_hbm(proj_in), in_hbm(proj_out))


def send_kernel(ext, own_hbm, near_lat_ref, far_lat_ref, near_ref, far_ref, sems):
    rows = own_hbm.shape[0]
    near = half_start(is_even("lon")) // HALF
    lat_even = is_even("lat")
    near_at = jnp.where(lat_even, rows - ext, 0)
    far_at = jnp.where(lat_even, 0, rows - ext)
    copies = []
    for ref, half in ((near_ref, near), (far_ref, 1 - near)):
        copies.append((own_hbm.at[:, half], ref))
    for ref, at in ((far_lat_ref, far_at), (near_lat_ref, near_at)):
        for n, half in enumerate((near, 1 - near)):
            copies.append((own_hbm.at[pl.ds(at, ext), half], ref.at[n]))
    copies = [pltpu.make_async_copy(src, dst, sems.at[n]) for n, (src, dst) in enumerate(copies)]
    for copy in copies:
        copy.start()
    for copy in copies:
        copy.wait()


def send(own, ext):
    rows, _, _, channels = own.shape
    shape = lambda *size: jax.ShapeDtypeStruct((*size, HALF, channels), own.dtype)
    return pl.pallas_call(
        functools.partial(send_kernel, ext),
        out_shape=(shape(2, ext), shape(2, ext), shape(rows), shape(rows)),
        in_specs=[pl.BlockSpec(memory_space=pl.ANY)],
        scratch_shapes=[pltpu.SemaphoreType.DMA((6,))],
        compiler_params=pltpu.CompilerParams(vmem_limit_bytes=SMALL), name="send",
    )(in_hbm(own))


def edge_kernel(far_lat_ref, near_lat_ref, near_ref, far_ref):
    lat_even = is_even("lat")
    ext = near_lat_ref.shape[1]
    for n, ref in enumerate((near_ref, far_ref)):
        far, near = far_lat_ref[n], near_lat_ref[n]
        ref[0:ext] = jnp.where(lat_even, far, near)
        ref[ext : 2 * ext] = jnp.where(lat_even, near, far)


def edges(far_lat, near_lat):
    _, ext, half, channels = far_lat.shape
    shape = jax.ShapeDtypeStruct((2 * ext, half, channels), far_lat.dtype)
    return pl.pallas_call(
        edge_kernel, out_shape=(shape, shape),
        compiler_params=pltpu.CompilerParams(vmem_limit_bytes=SMALL), name="edges",
    )(far_lat, near_lat)


def gelu(z):
    return (0.5 * z) * (1.0 + lax.erf(z * math.sqrt(0.5)))


def gather(pieces, start, size):
    parts, at = [], start
    while at < start + size:
        for ref, first, begin, length in pieces:
            if begin <= at < begin + length:
                count = min(start + size, begin + length) - at
                parts.append(ref[first + at - begin : first + at - begin + count, :])
                break
        else:
            later = [begin for _, _, begin, _ in pieces if begin > at]
            count = min([start + size, *later]) - at
            parts.append(pieces[0][0][0:count, :])
        at += count
    return parts[0] if len(parts) == 1 else jnp.concatenate(parts, axis=0)


def rows_kernel(block, starts, base, layout, extra, basis_near_ref, basis_far_ref, *refs):
    count = len(layout)
    fields, refs = refs[:count], refs[count:]
    mix_ref, gain_ref, bias_in_ref, bias_out_ref, proj_in, proj_out, *refs = refs
    refs = refs[extra:]
    near, far, side_near, side_far = (
        [(ref, *place) for ref, (kind, places) in zip(fields, layout) if kind == wanted for place in places]
        for wanted in range(4)
    )
    last = block > 0
    if last:
        out_hbm, normed, hidden, out_ref, sems = refs[-5:]
    else:
        *outs, normed, hidden = refs
    mix = [mix_ref[block, k : k + 1, :] for k in range(BASIS)]
    gain = gain_ref[block : block + 1, :]
    part, cells = SPAN * HALF, GROUP * HALF
    channels = proj_in.shape[0]
    for s, start in enumerate(starts):
        at = (start - LAT_REACH) * HALF
        both = [gather(near, at, part), gather(far, at, part)]
        for h, (basis_ref, side) in enumerate(((basis_near_ref, side_near), (basis_far_ref, side_far))):
            beside = gather(side, at, part)
            span = jnp.concatenate([*both, beside, beside[0 : DEPTH - 3 * part, :]], axis=0)
            parts = jnp.dot(basis_ref[(start - base) // GROUP], span, preferred_element_type=jnp.float32)
            conv = None
            for k in range(BASIS):
                term = parts[k * cells : (k + 1) * cells, :] * mix[k]
                conv = term if conv is None else conv + term
            mean = jnp.mean(conv, axis=-1, keepdims=True)
            centered = conv - mean
            variance = jnp.mean(centered * centered, axis=-1, keepdims=True)
            value = centered * lax.rsqrt(variance + NORM_EPS) * gain
            to = (h * len(starts) + s) * cells
            normed[to : to + cells, :] = value.astype(jnp.bfloat16)

    width = 256
    lhs = normed[...]
    for n in range(proj_in.shape[1] // width):
        at = slice(n * width, (n + 1) * width)
        z = jnp.dot(lhs, proj_in[:, at], preferred_element_type=jnp.float32) + bias_in_ref[block : block + 1, at]
        hidden[:, at] = gelu(z).astype(jnp.bfloat16)
    branch = jnp.dot(hidden[...], proj_out[...], preferred_element_type=jnp.float32)
    branch = branch + bias_out_ref[block : block + 1, :]
    for h, pieces in enumerate((near, far)):
        for s, start in enumerate(starts):
            at = (h * len(starts) + s) * cells
            own = gather(pieces, start * HALF, cells).astype(jnp.float32)
            value = (own + branch[at : at + cells, :]).astype(jnp.bfloat16)
            if last:
                out_ref[h, s * GROUP : (s + 1) * GROUP] = value.reshape(GROUP, HALF, channels)
            else:
                outs[h][s * cells : (s + 1) * cells, :] = value
    if last:
        near_half = half_start(is_even("lon")) // HALF
        copies = []
        for s, start in enumerate(starts):
            for h, half in enumerate((near_half, 1 - near_half)):
                copies.append(pltpu.make_async_copy(
                    out_ref.at[h, s * GROUP : (s + 1) * GROUP], out_hbm.at[start : start + GROUP, half],
                    sems.at[2 * s + h],
                ))
        for copy in copies:
            copy.start()
        for copy in copies:
            copy.wait()
    elif len(outs) == 4:
        lat = lax.axis_index("lat")
        rim = LAT_REACH * HALF
        for h in range(2):
            ref, message_ref = outs[h], outs[2 + h]
            for edge, at in ((0, 0), (lax.axis_size("lat") - 1, ref.shape[0] - cells)):
                @pl.when(lat == edge)
                def _():
                    ref[at : at + cells, :] = jnp.zeros((cells, channels), jnp.bfloat16)
            half, size = ref.shape[0] // 2, message_ref.shape[0] // 2
            message_ref[0:size, :] = ref[half - size : half, :]
            message_ref[size : 2 * size, :] = ref[half : half + size, :]


def run_rows(block, starts, base, basis, fields, weights, message=0, into=None, after=()):
    mix, gain, bias_in, bias_out, proj_in, proj_out = weights
    channels, hidden = proj_in.shape
    cells = len(starts) * GROUP * HALF
    vmem = pl.BlockSpec(memory_space=pltpu.VMEM)
    anywhere = pl.BlockSpec(memory_space=pl.ANY)
    scratch = [pltpu.VMEM((2 * cells, channels), jnp.bfloat16), pltpu.VMEM((2 * cells, hidden), jnp.bfloat16)]
    arrays = [*basis, *(array for array, _, _ in fields), mix, gain, bias_in, bias_out, proj_in, proj_out]
    layout = [(kind, places) for _, kind, places in fields]
    extra = list(after) if into is None else [*after, into[0]]
    if block > 0:
        rows = into[1]
        out_shape = jax.ShapeDtypeStruct((rows, 2, HALF, channels), jnp.bfloat16)
        out_specs = anywhere
        scratch += [
            pltpu.VMEM((2, len(starts) * GROUP, HALF, channels), jnp.bfloat16),
            pltpu.SemaphoreType.DMA((2 * len(starts),)),
        ]
        extra = [v for v in extra if v is not None]
    else:
        sizes = [cells] * 2 + ([message] * 2 if message else [])
        out_shape = tuple(jax.ShapeDtypeStruct((size, channels), jnp.bfloat16) for size in sizes)
        out_specs = (vmem,) * len(sizes)
    aliases = {len(arrays) + len(extra) - 1: 0} if into is not None and into[0] is not None else {}
    flops = 4 * cells * (2 * channels * hidden + 1024 * channels)
    return pl.pallas_call(
        functools.partial(rows_kernel, block, starts, base, layout, len(extra)),
        out_shape=out_shape,
        in_specs=[vmem] * len(arrays) + [anywhere] * len(extra),
        out_specs=out_specs,
        scratch_shapes=scratch,
        input_output_aliases=aliases,
        compiler_params=pltpu.CompilerParams(vmem_limit_bytes=16 << 20),
        cost_estimate=pl.CostEstimate(flops=flops, bytes_accessed=6 << 20, transcendentals=2 * cells * hidden),
        name=f"block{block}_{'outer' if min(starts) <= 0 else 'inner'}",
    )(*arrays, *extra)


def on_device(grid_field, conv_weight, norm_gain, proj_in, bias_in, proj_out, bias_out):
    lat_rows, lon_cells, channels = grid_field.shape
    lat_size, lon_size = lax.axis_size("lat"), lax.axis_size("lon")
    swap = lambda pairs: [(i, j) for a, b in pairs for i, j in ((a, b), (b, a))]
    lat_near = swap([(i, i + 1) for i in range(0, lat_size, 2)])
    lat_far = swap([(i, i + 1) for i in range(1, lat_size - 1, 2)])
    lon_near = swap([(i, i + 1) for i in range(0, lon_size, 2)])
    lon_far = swap([(i, (i + 1) % lon_size) for i in range(1, lon_size, 2)])

    own = grid_field.reshape(lat_rows, 2, HALF, channels)
    ext = 2 * LAT_REACH
    flat = lambda value: value.reshape(-1, channels)
    near_lat, far_lat, near, far = send(own, ext)
    near, far = flat(near), flat(far)
    side_near = lax.ppermute(near, "lon", lon_near)
    side_far = lax.ppermute(far, "lon", lon_far)
    far_lat = lax.ppermute(far_lat, "lat", lat_far)
    near_lat = lax.ppermute(near_lat, "lat", lat_near)
    near_edge, far_edge = (flat(value) for value in edges(far_lat, near_lat))
    side_near_edge = lax.ppermute(near_edge, "lon", lon_near)
    side_far_edge = lax.ppermute(far_edge, "lon", lon_far)
    windows = lat_rows // GROUP + 2
    base = -GROUP
    basis_near, basis_far, *projections = prepare(base, windows, lat_rows, near, proj_in, proj_out)
    basis = (basis_near, basis_far)
    small = (jnp.swapaxes(conv_weight, 1, 2), norm_gain, bias_in, bias_out)

    cells, rim = lat_rows * HALF, ext * HALF
    own_place = [(0, 0, cells)]
    edge_place = [(0, -rim, rim), (rim, cells, rim)]
    starts = list(range(base, lat_rows + 1, GROUP))
    fields = [(near, 0, own_place), (far, 1, own_place), (side_near, 2, own_place), (side_far, 3, own_place)]
    edge_fields = [
        (near_edge, 0, edge_place), (far_edge, 1, edge_place),
        (side_near_edge, 2, edge_place), (side_far_edge, 3, edge_place),
    ]
    weights = (*small, *projections[0:2])
    inner = [s for s in starts if s >= GROUP and s + 2 * GROUP <= lat_rows]
    outer = [s for s in starts if s not in inner]
    near_in, far_in = run_rows(0, inner, base, basis, fields, weights, after=(near_edge,))
    message = 2 * (GROUP + LAT_REACH) * HALF
    near_out, far_out, near_message, far_message = run_rows(
        0, outer, base, basis, fields + edge_fields, weights, message=message
    )
    side_near_in = lax.ppermute(near_in, "lon", lon_near)
    side_far_in = lax.ppermute(far_in, "lon", lon_far)
    side_near_out = lax.ppermute(near_message, "lon", lon_near)
    side_far_out = lax.ppermute(far_message, "lon", lon_far)

    begin, length = inner[0] * HALF, len(inner) * GROUP * HALF
    in_place = [(0, begin, length)]
    half = len(outer) * GROUP * HALF // 2
    out_place = [(0, begin - half, half), (half, begin + length, half)]
    size = message // 2
    message_place = [(0, begin - size, size), (size, begin + length, size)]
    fields = [(near_in, 0, in_place), (far_in, 1, in_place), (side_near_in, 2, in_place), (side_far_in, 3, in_place)]
    out_fields = [
        (near_out, 0, out_place), (far_out, 1, out_place),
        (side_near_out, 2, message_place), (side_far_out, 3, message_place),
    ]
    weights = (*small, *projections[2:4])
    starts = list(range(0, lat_rows, GROUP))
    core = [s for s in starts if s - LAT_REACH >= inner[0] and s + GROUP + LAT_REACH <= inner[-1] + GROUP]
    rest = [s for s in starts if s not in core]
    result = run_rows(1, core, base, basis, fields, weights, into=(None, lat_rows))
    result = run_rows(1, rest, base, basis, fields + out_fields, weights, into=(result, lat_rows))
    return result.reshape(grid_field.shape)


def solution(mesh):
    in_specs = (P("lat", "lon", None), P(), P(), P(), P(), P(), P())
    out_specs = P("lat", "lon", None)
    return jax.shard_map(
        on_device, mesh=mesh, in_specs=in_specs, out_specs=out_specs, check_vma=False
    )
```
